256 devices in a mesh: freq: 32 (over z, x), brow: 2 (over y_hi), bcol: 4 (over y_lo, core).
Axes of the slice: x: 4, y: 4 (y_hi: 2, y_lo: 2; y = y_hi * 2 + y_lo), z: 8, core: 2. Of those that a mesh axis runs over, the one named last changes fastest.
Arguments:
- voltages: bfloat16 [2, 1024, 94208], P(None, ('brow', 'bcol', 'freq')), may hold values from -6 to 6
- fir_taps: float32 [16, 4096], replicated, may hold values from -1.5 to 1.5
Outputs:
- visibilities: float32 [2, 128, 1024, 2, 4, 128], P(None, 'freq', 'brow', None, 'bcol')
The draws below stay inside these ranges and needn't reach their ends.
All inputs are finite; a program needn't handle non-finite values.
Results may differ from the reference program's by a relative error of at most 0.0036.
Values may be sent and summed in bfloat16 or wider, within the bound.
A program may use at most 64 MiB of HBM per device.

```python
import jax
import jax.numpy as jnp
from jax import lax

CHANNELS = 4096
RADIX = 64
TAPS = 16
AVG = 32
FRAMES = 8
STREAMS = 1024
SAMPLES = 94208
COARSE = 128
BLOCK = 128
N_BROW = 2
N_BCOL = 4


def level_of(key, dims, shards, smallest, top_value):
    factor_of, own = 1.0, jax.random.fold_in(key, 6)
    for position, shards_of in shards:
        steps = jnp.exp(jax.random.uniform(jax.random.fold_in(own, position), (shards_of,), jnp.float32, smallest / len(shards), top_value / len(shards)))
        factor_of = factor_of * jnp.repeat(steps, dims[position] // shards_of).reshape([-1 if axis == position else 1 for axis in range(len(dims))])
    return factor_of


def scatter_about(rng, shape, deviation, bound, pieces=(), held_as=jnp.bfloat16):
    result = deviation * jax.random.normal(rng, shape, jnp.float32)
    if pieces:
        result = result * level_of(rng, shape, pieces, -0.22, 0.18)
    return jnp.clip(result, -bound, bound).astype(held_as)


def setup_inputs(seed: int = 0) -> dict:
    key_list = jax.random.split(jax.random.key(seed), 3)
    return {
        "voltages": scatter_about(key_list[0], (2, STREAMS, SAMPLES), 1.0, 6.0, ((1, 256),)),
        "fir_taps": scatter_about(key_list[1], (TAPS, CHANNELS), 0.25, 1.5, (), jnp.float32),
    }


def channelize(block, fir_taps):
    width = block.shape[1]
    frames = block.astype(jnp.float32).reshape(2, width, FRAMES + TAPS - 1, CHANNELS)
    filtered = jnp.zeros((2, width, FRAMES, CHANNELS), jnp.float32)
    for tap in range(TAPS):
        filtered = filtered + fir_taps[tap] * frames[:, :, tap:tap + FRAMES, :]
    spectrum = jnp.fft.fft(filtered[0] + 1j * filtered[1], axis=-1) / RADIX
    parts = jnp.stack([jnp.real(spectrum), jnp.imag(spectrum)])
    return jnp.transpose(parts, (0, 1, 3, 2)).astype(jnp.bfloat16)


def reference(voltages, fir_taps):
    blocks = voltages.reshape(2, STREAMS // 64, 64, SAMPLES).transpose(1, 0, 2, 3)
    spectra = lax.map(lambda block: channelize(block, fir_taps), blocks)
    spectra = spectra.transpose(1, 0, 2, 3, 4).reshape(2, STREAMS, COARSE, AVG * FRAMES)
    scale = 1.0 / (FRAMES * AVG)

    def coarse_channel(index):
        block = lax.dynamic_index_in_dim(spectra, index, 2, keepdims=False)
        left = jnp.concatenate([block[0], block[1]], axis=1)
        flipped = jnp.concatenate([-block[1], block[0]], axis=1)
        real_part = jnp.dot(left, left.T, preferred_element_type=jnp.float32)
        imag_part = jnp.dot(left, flipped.T, preferred_element_type=jnp.float32)
        return jnp.stack([real_part, imag_part]) * scale

    vis = lax.map(coarse_channel, jnp.arange(COARSE, dtype=jnp.int32))
    vis = vis.transpose(1, 0, 2, 3)
    return vis.reshape(2, COARSE, STREAMS, N_BROW, N_BCOL, BLOCK)
```

```python
import functools
import math

import jax
import jax.numpy as jnp
import numpy as np
from jax import lax
from jax.experimental import pallas as pl
from jax.experimental.pallas import tpu as pltpu
from jax.sharding import PartitionSpec as P

CHANNELS = 4096
SCALE = 1.0 / 64.0
TAPS = 16
AVG = 32
FRAMES = 8
SLOW = 32
FAST = 128
WIDTH = 4
OWNED = 4
GROUPS = 32
KEPT = FRAMES * SLOW
ROWS = 2 * WIDTH
F32 = jnp.float32
BF16 = jnp.bfloat16


def halves(table):
    high = table.astype(np.float32).astype(jnp.bfloat16)
    low = (table - high.astype(np.float64)).astype(np.float32).astype(jnp.bfloat16)
    return high, low


def tables():
    b, k1 = np.arange(SLOW), np.arange(SLOW)
    angle = 2.0 * np.pi * (np.outer(k1, b) % SLOW) / SLOW
    first = np.zeros((2, WIDTH, SLOW, SLOW, 2, WIDTH))
    for s in range(WIDTH):
        first[0, s, :, :, 0, s] = np.cos(angle)
        first[0, s, :, :, 1, s] = np.sin(angle)
        first[1, s, :, :, 0, s] = -np.sin(angle)
        first[1, s, :, :, 1, s] = np.cos(angle)
    first = first.reshape(256, 256)
    n, m = np.arange(FAST), np.arange(FAST)
    angle = 2.0 * np.pi * (np.outer(m, n) % FAST) / FAST
    second = np.zeros((FAST, 2, 2, FAST))
    second[:, 0, 0, :] = np.cos(angle)
    second[:, 0, 1, :] = np.sin(angle)
    second[:, 1, 0, :] = -np.sin(angle)
    second[:, 1, 1, :] = np.cos(angle)
    second = second.reshape(256, 256) * SCALE
    angle = 2.0 * np.pi * np.outer(k1, n) / CHANNELS
    turn = np.stack([np.cos(angle), np.sin(angle)]).astype(np.float32)
    sort = np.zeros((2, GROUPS, WIDTH, GROUPS, 2, WIDTH), np.float32)
    for d in range(2):
        for g in range(GROUPS):
            for s in range(WIDTH):
                sort[d, g, s, g, d, s] = 1.0
    sort = sort.reshape(256, 256).astype(jnp.bfloat16)
    return np.stack(halves(first)), np.stack(halves(second)), turn, sort


FIRST, SECOND, TURN, SORT = tables()
NT = (((1,), (1,)), ((), ()))


def split(value):
    high = value.astype(BF16)
    low = (value - high.astype(F32)).astype(BF16)
    return high, low


def channelize_kernel(x_ref, taps_ref, first_ref, second_ref, turn_ref, out_ref, fir, spread):
    def column(b, carry):
        lanes = pl.multiple_of(b * FAST, FAST)
        rows = pl.multiple_of(b * ROWS, ROWS)
        frames = []
        for j in range(FRAMES + TAPS - 1):
            at = pl.multiple_of(j * CHANNELS + lanes, FAST)
            real = x_ref[0, :, pl.ds(at, FAST)].astype(F32)
            imag = x_ref[1, :, pl.ds(at, FAST)].astype(F32)
            frames.append(jnp.concatenate([real, imag], axis=0))
        taps = [taps_ref[pl.ds(p, 1), pl.ds(lanes, FAST)] for p in range(TAPS)]
        for t in range(FRAMES):
            total = taps[0] * frames[t]
            for p in range(1, TAPS):
                total = total + taps[p] * frames[t + p]
            fir[pl.ds(rows, ROWS), t * FAST:(t + 1) * FAST] = total
        return carry

    lax.fori_loop(0, SLOW, column, 0)
    high, low = split(fir[...])
    dot = functools.partial(jnp.dot, preferred_element_type=F32)
    section = dot(first_ref[0], high) + dot(first_ref[1], high) + dot(first_ref[0], low)
    cosine, sine = turn_ref[0], turn_ref[1]
    for s in range(WIDTH):
        parts = []
        for t in range(FRAMES):
            real = section[s * SLOW:(s + 1) * SLOW, t * FAST:(t + 1) * FAST]
            imag = section[128 + s * SLOW:128 + (s + 1) * SLOW, t * FAST:(t + 1) * FAST]
            parts.append(jnp.concatenate([real * cosine + imag * sine, imag * cosine - real * sine], axis=1))
        high, low = split(jnp.concatenate(parts, axis=0))
        dot_nt = functools.partial(lax.dot_general, dimension_numbers=NT, preferred_element_type=F32)
        spectrum = dot_nt(second_ref[0], high) + dot_nt(second_ref[1], high) + dot_nt(second_ref[0], low)
        for half in range(2):
            lanes = slice(half * 128, (half + 1) * 128)
            spread[half, pl.ds(s, 256, stride=WIDTH), :] = spectrum[:, lanes]
    for half in range(2):
        out_ref[:, half * 128:(half + 1) * 128] = spread[half].astype(BF16)


def channelize(voltages, fir_taps):
    vmem = pl.BlockSpec(memory_space=pltpu.VMEM)
    return pl.pallas_call(
        channelize_kernel,
        out_shape=jax.ShapeDtypeStruct((GROUPS * OWNED * ROWS, KEPT), BF16),
        in_specs=[vmem] * 5,
        out_specs=vmem,
        scratch_shapes=[
            pltpu.VMEM((256, FRAMES * FAST), F32),
            pltpu.VMEM((2, GROUPS * OWNED * ROWS, 128), F32),
        ],
        name="channelize",
    )(voltages, fir_taps, jnp.asarray(FIRST), jnp.asarray(SECOND), jnp.asarray(TURN))


def correlate_kernel(slots_ref, left_ref, first_ref, second_ref, sort_ref, out_ref):
    del slots_ref
    sort = sort_ref[...]
    sorted_blocks = [
        jnp.dot(sort, ref[0, 0], preferred_element_type=F32).astype(BF16) for ref in (first_ref, second_ref)
    ]
    right = jnp.concatenate(
        [sorted_blocks[0][:128], sorted_blocks[1][:128], sorted_blocks[0][128:], sorted_blocks[1][128:]], axis=0
    )
    upper = lax.broadcasted_iota(jnp.int32, (GROUPS, ROWS, 256), 1) < WIDTH
    for block in range(left_ref.shape[0]):
        product = lax.dot_general(left_ref[block, 0], right, NT, preferred_element_type=F32)
        with_real = product[:, :256].reshape(GROUPS, ROWS, 256)
        with_imag = pltpu.roll(product[:, 256:].reshape(GROUPS, ROWS, 256), WIDTH, axis=1)
        mixed = (with_real + jnp.where(upper, with_imag, -with_imag)) * (1.0 / (FRAMES * AVG))
        pairs = mixed.reshape(GROUPS // 2, 2, ROWS, 256)
        even, odd = pairs[:, 0], pairs[:, 1]
        real = jnp.where(upper[:GROUPS // 2], even, pltpu.roll(odd, WIDTH, axis=1)).reshape(128, 256)
        imag = jnp.where(upper[:GROUPS // 2], pltpu.roll(even, WIDTH, axis=1), odd).reshape(128, 256)
        for r in range(2):
            rows = pl.ds(block * 256 + r, 128, stride=2)
            out_ref[0, 0, rows, :] = real[:, r * 128:(r + 1) * 128]
            out_ref[1, 0, rows, :] = imag[:, r * 128:(r + 1) * 128]


def correlate(blocks, slots):
    grid_spec = pltpu.PrefetchScalarGridSpec(
        num_scalar_prefetch=1,
        grid=(OWNED,),
        in_specs=[
            pl.BlockSpec((4, 1, 256, KEPT), lambda q, slots: (0, q, 0, 0)),
            pl.BlockSpec((1, 1, 256, KEPT), lambda q, slots: (slots[0], q, 0, 0)),
            pl.BlockSpec((1, 1, 256, KEPT), lambda q, slots: (slots[1], q, 0, 0)),
            pl.BlockSpec((256, 256), lambda q, slots: (0, 0)),
        ],
        out_specs=pl.BlockSpec((2, 1, 1024, 128), lambda q, slots: (0, q, 0, 0)),
    )
    return pl.pallas_call(
        correlate_kernel,
        grid_spec=grid_spec,
        out_shape=jax.ShapeDtypeStruct((2, OWNED, 1024, 128), F32),
        name="correlate",
    )(slots, blocks, blocks, blocks, jnp.asarray(SORT))


def exchange(spectra):
    owned = lax.all_to_all(spectra.reshape(GROUPS, OWNED, ROWS, KEPT), "freq", split_axis=0, concat_axis=0, tiled=True)
    owned = owned.transpose(1, 0, 2, 3).reshape(OWNED, 256, KEPT)
    left = lax.all_gather(owned, "bcol", axis=0)
    right = lax.all_gather(owned, "brow", axis=0)
    other = lax.dynamic_index_in_dim(right, 1 - lax.axis_index("brow"), 0)
    return jnp.concatenate([left, other], axis=0)


def shards(voltages, fir_taps):
    spectra = channelize(voltages, fir_taps)
    blocks = exchange(spectra)
    brow, bcol = lax.axis_index("brow"), lax.axis_index("bcol")
    slots = jnp.stack([bcol + brow * (4 - bcol), 4 - brow * (4 - bcol)]).astype(jnp.int32)
    result = correlate(blocks, slots)
    return result.reshape(2, OWNED, 512, 2, 1, 128)


def solution(mesh):
    in_specs = (P(None, ("brow", "bcol", "freq"), None), P())
    out_specs = P(None, "freq", "brow", None, "bcol", None)
    return jax.shard_map(shards, mesh=mesh, in_specs=in_specs, out_specs=out_specs, check_vma=False)
```

```python
import functools
import math

import jax
import jax.numpy as jnp
import numpy as np
from jax import lax
from jax.experimental import pallas as pl
from jax.experimental.pallas import tpu as pltpu
from jax.sharding import PartitionSpec as P

CHANNELS = 4096
SCALE = 1.0 / 64.0
TAPS = 16
AVG = 32
FRAMES = 8
SLOW = 32
FAST = 128
WIDTH = 4
OWNED = 4
GROUPS = 32
KEPT = FRAMES * SLOW
ROWS = 2 * WIDTH
N_X = 4
N_Z = 8
N_BCOL = 4
MESH = pl.DeviceIdType.MESH
F32 = jnp.float32
BF16 = jnp.bfloat16


def halves(table):
    high = table.astype(np.float32).astype(jnp.bfloat16)
    low = (table - high.astype(np.float64)).astype(np.float32).astype(jnp.bfloat16)
    return high, low


def tables():
    b, k1 = np.arange(SLOW), np.arange(SLOW)
    angle = 2.0 * np.pi * (np.outer(k1, b) % SLOW) / SLOW
    first = np.zeros((2, WIDTH, SLOW, SLOW, 2, WIDTH))
    for s in range(WIDTH):
        first[0, s, :, :, 0, s] = np.cos(angle)
        first[0, s, :, :, 1, s] = np.sin(angle)
        first[1, s, :, :, 0, s] = -np.sin(angle)
        first[1, s, :, :, 1, s] = np.cos(angle)
    first = first.reshape(256, 256)
    n, m = np.arange(FAST), np.arange(FAST)
    angle = 2.0 * np.pi * (np.outer(m, n) % FAST) / FAST
    second = np.zeros((FAST, 2, 2, FAST))
    second[:, 0, 0, :] = np.cos(angle)
    second[:, 0, 1, :] = np.sin(angle)
    second[:, 1, 0, :] = -np.sin(angle)
    second[:, 1, 1, :] = np.cos(angle)
    second = second.reshape(256, 256) * SCALE
    angle = 2.0 * np.pi * np.outer(k1, n) / CHANNELS
    turn = np.stack([np.cos(angle), np.sin(angle)]).astype(np.float32)
    sort = np.zeros((2, GROUPS, WIDTH, GROUPS, 2, WIDTH), np.float32)
    for d in range(2):
        for g in range(GROUPS):
            for s in range(WIDTH):
                sort[d, g, s, g, d, s] = 1.0
    sort = sort.reshape(256, 256).astype(jnp.bfloat16)
    return np.stack(halves(first)), np.stack(halves(second)), turn, sort


FIRST, SECOND, TURN, SORT = tables()
NT = (((1,), (1,)), ((), ()))


def split(value):
    high = value.astype(BF16)
    low = (value - high.astype(F32)).astype(BF16)
    return high, low


def channelize_kernel(x_ref, taps_ref, first_ref, second_ref, turn_ref, out_ref, fir, spread):
    def column(b, carry):
        lanes = pl.multiple_of(b * FAST, FAST)
        rows = pl.multiple_of(b * ROWS, ROWS)
        frames = []
        for j in range(FRAMES + TAPS - 1):
            at = pl.multiple_of(j * CHANNELS + lanes, FAST)
            real = x_ref[0, :, pl.ds(at, FAST)].astype(F32)
            imag = x_ref[1, :, pl.ds(at, FAST)].astype(F32)
            frames.append(jnp.concatenate([real, imag], axis=0))
        taps = [taps_ref[pl.ds(p, 1), pl.ds(lanes, FAST)] for p in range(TAPS)]
        for t in range(FRAMES):
            total = taps[0] * frames[t]
            for p in range(1, TAPS):
                total = total + taps[p] * frames[t + p]
            fir[pl.ds(rows, ROWS), t * FAST:(t + 1) * FAST] = total
        return carry

    lax.fori_loop(0, SLOW, column, 0)
    high, low = split(fir[...])
    dot = functools.partial(jnp.dot, preferred_element_type=F32)
    section = dot(first_ref[0], high) + dot(first_ref[1], high) + dot(first_ref[0], low)
    cosine, sine = turn_ref[0], turn_ref[1]
    for s in range(WIDTH):
        parts = []
        for t in range(FRAMES):
            real = section[s * SLOW:(s + 1) * SLOW, t * FAST:(t + 1) * FAST]
            imag = section[128 + s * SLOW:128 + (s + 1) * SLOW, t * FAST:(t + 1) * FAST]
            parts.append(jnp.concatenate([real * cosine + imag * sine, imag * cosine - real * sine], axis=1))
        high, low = split(jnp.concatenate(parts, axis=0))
        dot_nt = functools.partial(lax.dot_general, dimension_numbers=NT, preferred_element_type=F32)
        spectrum = dot_nt(second_ref[0], high) + dot_nt(second_ref[1], high) + dot_nt(second_ref[0], low)
        for half in range(2):
            lanes = slice(half * 128, (half + 1) * 128)
            spread[half, pl.ds(s, 256, stride=WIDTH), :] = spectrum[:, lanes]
    for half in range(2):
        out_ref[:, half * 128:(half + 1) * 128] = spread[half].astype(BF16)


def channelize(voltages, fir_taps):
    vmem = pl.BlockSpec(memory_space=pltpu.VMEM)
    return pl.pallas_call(
        channelize_kernel,
        out_shape=jax.ShapeDtypeStruct((GROUPS * OWNED * ROWS, KEPT), BF16),
        in_specs=[vmem] * 5,
        out_specs=vmem,
        scratch_shapes=[
            pltpu.VMEM((256, FRAMES * FAST), F32),
            pltpu.VMEM((2, GROUPS * OWNED * ROWS, 128), F32),
        ],
        name="channelize",
    )(voltages, fir_taps, jnp.asarray(FIRST), jnp.asarray(SECOND), jnp.asarray(TURN))


def correlate_kernel(slots_ref, left_ref, first_ref, second_ref, sort_ref, out_ref):
    del slots_ref
    sort = sort_ref[...]
    sorted_blocks = [
        jnp.dot(sort, ref[0, 0], preferred_element_type=F32).astype(BF16) for ref in (first_ref, second_ref)
    ]
    right = jnp.concatenate(
        [sorted_blocks[0][:128], sorted_blocks[1][:128], sorted_blocks[0][128:], sorted_blocks[1][128:]], axis=0
    )
    upper = lax.broadcasted_iota(jnp.int32, (GROUPS, ROWS, 256), 1) < WIDTH
    for block in range(left_ref.shape[0]):
        product = lax.dot_general(left_ref[block, 0], right, NT, preferred_element_type=F32)
        with_real = product[:, :256].reshape(GROUPS, ROWS, 256)
        with_imag = pltpu.roll(product[:, 256:].reshape(GROUPS, ROWS, 256), WIDTH, axis=1)
        mixed = (with_real + jnp.where(upper, with_imag, -with_imag)) * (1.0 / (FRAMES * AVG))
        pairs = mixed.reshape(GROUPS // 2, 2, ROWS, 256)
        even, odd = pairs[:, 0], pairs[:, 1]
        real = jnp.where(upper[:GROUPS // 2], even, pltpu.roll(odd, WIDTH, axis=1)).reshape(128, 256)
        imag = jnp.where(upper[:GROUPS // 2], pltpu.roll(even, WIDTH, axis=1), odd).reshape(128, 256)
        for r in range(2):
            rows = pl.ds(block * 256 + r, 128, stride=2)
            out_ref[0, 0, rows, :] = real[:, r * 128:(r + 1) * 128]
            out_ref[1, 0, rows, :] = imag[:, r * 128:(r + 1) * 128]


def correlate(blocks, slots):
    grid_spec = pltpu.PrefetchScalarGridSpec(
        num_scalar_prefetch=1,
        grid=(OWNED,),
        in_specs=[
            pl.BlockSpec((4, 1, 256, KEPT), lambda q, slots: (0, q, 0, 0)),
            pl.BlockSpec((1, 1, 256, KEPT), lambda q, slots: (slots[0], q, 0, 0)),
            pl.BlockSpec((1, 1, 256, KEPT), lambda q, slots: (slots[1], q, 0, 0)),
            pl.BlockSpec((256, 256), lambda q, slots: (0, 0)),
        ],
        out_specs=pl.BlockSpec((2, 1, 1024, 128), lambda q, slots: (0, q, 0, 0)),
    )
    return pl.pallas_call(
        correlate_kernel,
        grid_spec=grid_spec,
        out_shape=jax.ShapeDtypeStruct((2, OWNED, 1024, 128), F32),
        name="correlate",
    )(slots, blocks, blocks, blocks, jnp.asarray(SORT))


def exchange_kernel(
    spectra, blocks, local, turn_send, turn_recv, near_send, core_send, relay_send, far_send, near_recv, core_recv,
    relay_recv, far_recv
):
    freq, brow, bcol = lax.axis_index("freq"), lax.axis_index("brow"), lax.axis_index("bcol")
    z, x = freq // N_X, freq % N_X
    y_low, core = bcol // 2, bcol % 2
    other_core = 2 * y_low + 1 - core
    near = 2 * (1 - y_low) + core

    barrier = pltpu.get_barrier_semaphore()

    def greet(i, carry):
        pl.semaphore_signal(barrier, inc=1, device_id=((freq + i) % GROUPS, brow, bcol), device_id_type=MESH)
        return carry

    lax.fori_loop(1, GROUPS, greet, 0)
    for peer in ((freq, brow, other_core), (freq, brow, near), (freq, 1 - brow, near)):
        pl.semaphore_signal(barrier, inc=1, device_id=peer, device_id_type=MESH)
    pl.semaphore_wait(barrier, GROUPS - 1 + 3)

    def shift(j):
        return (N_Z + ((j + 1) // 2) * (2 * (j % 2) - 1)) % N_Z

    def chunk(slot, j):
        return blocks.at[slot, :, pl.ds((z + N_Z - shift(j)) % N_Z * N_X, N_X)]

    def turn(j, dx):
        target = (z + shift(j)) % N_Z * N_X + (x + dx) % N_X
        pltpu.make_async_remote_copy(
            src_ref=spectra.at[target], dst_ref=blocks.at[bcol, :, freq], send_sem=turn_send, recv_sem=turn_recv.at[j],
            device_id=(target, brow, bcol), device_id_type=MESH,
        ).start()

    def pass_on(source, target, peer, send, recv):
        pltpu.make_async_remote_copy(
            src_ref=source, dst_ref=target, send_sem=send, recv_sem=recv, device_id=peer, device_id_type=MESH
        ).start()

    def arrived(ref, semaphore):
        pltpu.make_async_copy(ref, ref, semaphore).wait()

    own = pltpu.make_async_copy(spectra.at[freq], blocks.at[bcol, :, freq], local)
    own.start()
    for dx in range(1, N_X):
        turn(0, dx)

    def send_row(j, carry):
        for dx in range(N_X):
            turn(j, dx)
        return carry

    lax.fori_loop(1, N_Z, send_row, 0)

    def spread_own(j):
        held = chunk(bcol, j)
        pass_on(held, held, (freq, brow, near), near_send, near_recv.at[j])
        pass_on(held, held, (freq, brow, other_core), core_send, core_recv)

    def spread_near(j):
        held = chunk(near, j)
        arrived(held, near_recv.at[j])
        pass_on(held, held, (freq, brow, other_core), relay_send, relay_recv)
        pass_on(held, chunk(N_BCOL, j), (freq, 1 - brow, near), far_send, far_recv)

    own.wait()
    arrived(blocks.at[bcol, :, pl.ds(0, N_X - 1)], turn_recv.at[0])
    spread_own(0)

    def row(j, carry):
        arrived(chunk(bcol, j), turn_recv.at[j])
        spread_own(j)
        spread_near(j - 1)
        return carry

    lax.fori_loop(1, N_Z, row, 0)
    spread_near(N_Z - 1)
    arrived(spectra.at[pl.ds(0, GROUPS - 1)], turn_send)
    for semaphore in (near_send, core_send, relay_send, far_send, core_recv, relay_recv, far_recv):
        arrived(blocks.at[0], semaphore)


def exchange(spectra):
    anywhere = pl.BlockSpec(memory_space=pl.ANY)
    dma = pltpu.SemaphoreType.DMA
    blocks = pl.pallas_call(
        exchange_kernel,
        out_shape=jax.ShapeDtypeStruct((N_BCOL + 1, OWNED, GROUPS, ROWS, KEPT), BF16),
        in_specs=[anywhere],
        out_specs=anywhere,
        scratch_shapes=[dma, dma, dma((N_Z,)), dma, dma, dma, dma, dma((N_Z,)), dma, dma, dma],
        compiler_params=pltpu.CompilerParams(collective_id=0, has_side_effects=True),
        name="exchange",
    )(spectra.reshape(GROUPS, OWNED, ROWS, KEPT))
    return blocks.reshape(N_BCOL + 1, OWNED, GROUPS * ROWS, KEPT)


def shards(voltages, fir_taps):
    spectra = channelize(voltages, fir_taps)
    blocks = exchange(spectra)
    brow, bcol = lax.axis_index("brow"), lax.axis_index("bcol")
    slots = jnp.stack([bcol + brow * (4 - bcol), 4 - brow * (4 - bcol)]).astype(jnp.int32)
    result = correlate(blocks, slots)
    return result.reshape(2, OWNED, 512, 2, 1, 128)


def solution(mesh):
    in_specs = (P(None, ("brow", "bcol", "freq"), None), P())
    out_specs = P(None, "freq", "brow", None, "bcol", None)
    return jax.shard_map(shards, mesh=mesh, in_specs=in_specs, out_specs=out_specs, check_vma=False)
```

```python
import functools
import math

import jax
import jax.numpy as jnp
import numpy as np
from jax import lax
from jax.experimental import pallas as pl
from jax.experimental.pallas import tpu as pltpu
from jax.sharding import PartitionSpec as P

CHANNELS = 4096
SCALE = 1.0 / 64.0
TAPS = 16
AVG = 32
FRAMES = 8
SLOW = 32
FAST = 128
WIDTH = 4
OWNED = 4
GROUPS = 32
KEPT = FRAMES * SLOW
ROWS = 2 * WIDTH
N_X = 4
N_Z = 8
N_BCOL = 4
MESH = pl.DeviceIdType.MESH
F32 = jnp.float32
BF16 = jnp.bfloat16


def halves(table):
    high = table.astype(np.float32).astype(jnp.bfloat16)
    low = (table - high.astype(np.float64)).astype(np.float32).astype(jnp.bfloat16)
    return high, low


def tables():
    b, k1 = np.arange(SLOW), np.arange(SLOW)
    angle = 2.0 * np.pi * (np.outer(k1, b) % SLOW) / SLOW
    first = np.zeros((2, WIDTH, SLOW, SLOW, 2, WIDTH))
    for s in range(WIDTH):
        first[0, s, :, :, 0, s] = np.cos(angle)
        first[0, s, :, :, 1, s] = np.sin(angle)
        first[1, s, :, :, 0, s] = -np.sin(angle)
        first[1, s, :, :, 1, s] = np.cos(angle)
    first = first.reshape(256, 256)
    n, m = np.arange(FAST), np.arange(FAST)
    angle = 2.0 * np.pi * (np.outer(m, n) % FAST) / FAST
    second = np.zeros((FAST, 2, 2, FAST))
    second[:, 0, 0, :] = np.cos(angle)
    second[:, 0, 1, :] = np.sin(angle)
    second[:, 1, 0, :] = -np.sin(angle)
    second[:, 1, 1, :] = np.cos(angle)
    second = second.reshape(256, 256) * SCALE
    angle = 2.0 * np.pi * np.outer(k1, n) / CHANNELS
    turn = np.stack([np.cos(angle), np.sin(angle)]).astype(np.float32)
    sort = np.zeros((2, GROUPS, WIDTH, GROUPS, 2, WIDTH), np.float32)
    for d in range(2):
        for g in range(GROUPS):
            for s in range(WIDTH):
                sort[d, g, s, g, d, s] = 1.0
    sort = sort.reshape(256, 256).astype(jnp.bfloat16)
    return np.stack(halves(first)), np.stack(halves(second)), turn, sort


FIRST, SECOND, TURN, SORT = tables()
NT = (((1,), (1,)), ((), ()))


def split(value):
    high = value.astype(BF16)
    low = (value - high.astype(F32)).astype(BF16)
    return high, low


def channelize(load, taps_ref, first_ref, second_ref, turn_ref, spectra, fir, spread):
    def column(b, carry):
        lanes = pl.multiple_of(b * FAST, FAST)
        rows = pl.multiple_of(b * ROWS, ROWS)
        frames = []
        for j in range(FRAMES + TAPS - 1):
            real, imag = load(pl.multiple_of(j * CHANNELS + lanes, FAST))
            frames.append(jnp.concatenate([real.astype(F32), imag.astype(F32)], axis=0))
        taps = [taps_ref[pl.ds(p, 1), pl.ds(lanes, FAST)] for p in range(TAPS)]
        for t in range(FRAMES):
            total = taps[0] * frames[t]
            for p in range(1, TAPS):
                total = total + taps[p] * frames[t + p]
            fir[pl.ds(rows, ROWS), t * FAST:(t + 1) * FAST] = total
        return carry

    lax.fori_loop(0, SLOW, column, 0, unroll=4)
    high, low = split(fir[...])
    dot = functools.partial(jnp.dot, preferred_element_type=F32)
    section = dot(first_ref[0], high) + dot(first_ref[1], high) + dot(first_ref[0], low)
    cosine, sine = turn_ref[0], turn_ref[1]
    for s in range(WIDTH):
        parts = []
        for t in range(FRAMES):
            real = section[s * SLOW:(s + 1) * SLOW, t * FAST:(t + 1) * FAST]
            imag = section[128 + s * SLOW:128 + (s + 1) * SLOW, t * FAST:(t + 1) * FAST]
            parts.append(jnp.concatenate([real * cosine + imag * sine, imag * cosine - real * sine], axis=1))
        high, low = split(jnp.concatenate(parts, axis=0))
        dot_nt = functools.partial(lax.dot_general, dimension_numbers=NT, preferred_element_type=F32)
        spectrum = dot_nt(second_ref[0], high) + dot_nt(second_ref[1], high) + dot_nt(second_ref[0], low)
        for half in range(2):
            lanes = slice(half * 128, (half + 1) * 128)
            spread[half, pl.ds(s, 256, stride=WIDTH), :] = spectrum[:, lanes]
    for half in range(2):
        lanes = slice(half * 128, (half + 1) * 128)
        spectra[:, :, :, lanes] = spread[half].reshape(GROUPS, OWNED, ROWS, 128).astype(BF16)


SCHEDULE = tuple((k[0], int(k[1])) for k in ("o0", "o1", "n0", "o2", "o3", "n1", "o4", "o5", "n2", "o6", "n3", "o7", "n4", "n5", "n6", "n7"))


def spectra_kernel(
    x_hbm, taps_hbm, first_hbm, second_hbm, turn_hbm, blocks, x_ref, taps_ref, first_ref, second_ref, turn_ref, fir, spread,
    spectra, load_sem, local, turn_send, turn_recv, near_send, core_send, relay_send, far_send, near_recv, core_recv,
    relay_recv, far_recv
):
    loads = [
        pltpu.make_async_copy(source, target, load_sem.at[i])
        for i, (source, target) in enumerate(
            ((x_hbm, x_ref), (taps_hbm, taps_ref), (first_hbm, first_ref), (second_hbm, second_ref), (turn_hbm, turn_ref))
        )
    ]
    for copy in loads:
        copy.start()

    freq, brow, bcol = lax.axis_index("freq"), lax.axis_index("brow"), lax.axis_index("bcol")
    z, x = freq // N_X, freq % N_X
    y_low, core = bcol // 2, bcol % 2
    other_core = 2 * y_low + 1 - core
    near = 2 * (1 - y_low) + core

    barrier = pltpu.get_barrier_semaphore()

    def greet(i, carry):
        pl.semaphore_signal(barrier, inc=1, device_id=((freq + i) % GROUPS, brow, bcol), device_id_type=MESH)
        return carry

    lax.fori_loop(1, GROUPS, greet, 0)
    for peer in ((freq, brow, other_core), (freq, brow, near), (freq, 1 - brow, near)):
        pl.semaphore_signal(barrier, inc=1, device_id=peer, device_id_type=MESH)

    for copy in loads:
        copy.wait()

    def load(at):
        return x_ref[0, :, pl.ds(at, FAST)], x_ref[1, :, pl.ds(at, FAST)]

    channelize(load, taps_ref, first_ref, second_ref, turn_ref, spectra, fir, spread)
    pl.semaphore_wait(barrier, GROUPS - 1 + 3)

    def shift(j):
        return (N_Z + ((j + 1) // 2) * (2 * (j % 2) - 1)) % N_Z

    def chunk(slot, j):
        return blocks.at[slot, :, pl.ds((z + N_Z - shift(j)) % N_Z * N_X, N_X)]

    def turn(j, dx):
        target = (z + shift(j)) % N_Z * N_X + (x + dx) % N_X
        pltpu.make_async_remote_copy(
            src_ref=spectra.at[target], dst_ref=blocks.at[bcol, :, freq], send_sem=turn_send, recv_sem=turn_recv.at[j],
            device_id=(target, brow, bcol), device_id_type=MESH,
        ).start()

    def pass_on(source, target, peer, send, recv):
        pltpu.make_async_remote_copy(
            src_ref=source, dst_ref=target, send_sem=send, recv_sem=recv, device_id=peer, device_id_type=MESH
        ).start()

    def arrived(ref, semaphore):
        pltpu.make_async_copy(ref, ref, semaphore).wait()

    own = pltpu.make_async_copy(spectra.at[freq], blocks.at[bcol, :, freq], local)
    own.start()
    for dx in range(1, N_X):
        turn(0, dx)

    def send_row(j, carry):
        for dx in range(N_X):
            turn(j, dx)
        return carry

    lax.fori_loop(1, N_Z, send_row, 0)

    def spread_own(j):
        if j == 0:
            own.wait()
            arrived(blocks.at[bcol, :, pl.ds(0, N_X - 1)], turn_recv.at[0])
        else:
            arrived(chunk(bcol, j), turn_recv.at[j])
        held = chunk(bcol, j)
        pass_on(held, held, (freq, brow, near), near_send, near_recv.at[j])
        pass_on(held, held, (freq, brow, other_core), core_send, core_recv)

    def spread_near(j):
        held = chunk(near, j)
        arrived(held, near_recv.at[j])
        pass_on(held, chunk(N_BCOL, j), (freq, 1 - brow, near), far_send, far_recv)
        pass_on(held, held, (freq, brow, other_core), relay_send, relay_recv)

    for kind, j in SCHEDULE:
        (spread_own if kind == "o" else spread_near)(j)
    arrived(spectra.at[pl.ds(0, GROUPS - 1)], turn_send)
    for semaphore in (near_send, core_send, relay_send, far_send, core_recv, relay_recv, far_recv):
        arrived(blocks.at[0], semaphore)


def spread_spectra(voltages, fir_taps):
    anywhere = pl.BlockSpec(memory_space=pl.ANY)
    dma = pltpu.SemaphoreType.DMA
    blocks = pl.pallas_call(
        spectra_kernel,
        out_shape=jax.ShapeDtypeStruct((N_BCOL + 1, OWNED, GROUPS, ROWS, KEPT), BF16),
        in_specs=[pl.BlockSpec(memory_space=pltpu.HBM)] * 5,
        out_specs=anywhere,
        scratch_shapes=[
            pltpu.VMEM(voltages.shape, BF16),
            pltpu.VMEM(fir_taps.shape, F32),
            pltpu.VMEM(FIRST.shape, BF16),
            pltpu.VMEM(SECOND.shape, BF16),
            pltpu.VMEM(TURN.shape, F32),
            pltpu.VMEM((256, FRAMES * FAST), F32),
            pltpu.VMEM((2, GROUPS * OWNED * ROWS, 128), F32),
            pltpu.VMEM((GROUPS, OWNED, ROWS, KEPT), BF16),
            dma((5,)), dma, dma, dma((N_Z,)), dma, dma, dma, dma, dma((N_Z,)), dma, dma, dma,
        ],
        compiler_params=pltpu.CompilerParams(collective_id=0, has_side_effects=True, vmem_limit_bytes=24 * 2**20),
        name="spectra",
    )(*[pltpu.with_memory_space_constraint(v, pltpu.HBM) for v in (voltages, fir_taps, jnp.asarray(FIRST), jnp.asarray(SECOND), jnp.asarray(TURN))])
    return blocks.reshape(N_BCOL + 1, OWNED, GROUPS * ROWS, KEPT)


def correlate_kernel(held, sort_ref, out, built, store_sem):
    brow, bcol = lax.axis_index("brow"), lax.axis_index("bcol")
    slots = (bcol + brow * (N_BCOL - bcol), N_BCOL - brow * (N_BCOL - bcol))
    upper = lax.broadcasted_iota(jnp.int32, (GROUPS, ROWS, 256), 1) < WIDTH
    stores = []
    for q in range(OWNED):
        sort = sort_ref[...]
        parts = [jnp.dot(sort, held[slot, q], preferred_element_type=F32).astype(BF16) for slot in slots]
        right = jnp.concatenate([parts[0][:128], parts[1][:128], parts[0][128:], parts[1][128:]], axis=0)
        for block in range(N_BCOL):
            product = lax.dot_general(held[block, q], right, NT, preferred_element_type=F32)
            with_real = product[:, :256].reshape(GROUPS, ROWS, 256)
            with_imag = pltpu.roll(product[:, 256:].reshape(GROUPS, ROWS, 256), WIDTH, axis=1)
            mixed = (with_real + jnp.where(upper, with_imag, -with_imag)) * (1.0 / (FRAMES * AVG))
            pairs = mixed.reshape(GROUPS // 2, 2, ROWS, 256)
            even, odd = pairs[:, 0], pairs[:, 1]
            real = jnp.where(upper[:GROUPS // 2], even, pltpu.roll(odd, WIDTH, axis=1)).reshape(128, 256)
            imag = jnp.where(upper[:GROUPS // 2], pltpu.roll(even, WIDTH, axis=1), odd).reshape(128, 256)
            for r in range(2):
                rows = pl.ds(block * 256 + r, 128, stride=2)
                built[0, q, rows, :] = real[:, r * 128:(r + 1) * 128]
                built[1, q, rows, :] = imag[:, r * 128:(r + 1) * 128]
            part = (slice(None), q, pl.ds(block * 256, 256))
            stores.append(pltpu.make_async_copy(built.at[part], out.at[part], store_sem.at[q, block]))
            stores[-1].start()
    for copy in stores:
        copy.wait()


def correlate(blocks):
    vmem = pl.BlockSpec(memory_space=pltpu.VMEM)
    shape = (2, OWNED, 1024, 128)
    return pl.pallas_call(
        correlate_kernel,
        out_shape=jax.ShapeDtypeStruct(shape, F32),
        in_specs=[vmem] * 2,
        out_specs=pl.BlockSpec(memory_space=pltpu.HBM),
        scratch_shapes=[pltpu.VMEM(shape, F32), pltpu.SemaphoreType.DMA((OWNED, N_BCOL))],
        compiler_params=pltpu.CompilerParams(vmem_limit_bytes=24 * 2**20),
        name="correlate",
    )(blocks, jnp.asarray(SORT))


def shards(voltages, fir_taps):
    blocks = spread_spectra(voltages, fir_taps)
    return correlate(blocks).reshape(2, OWNED, 512, 2, 1, 128)


def solution(mesh):
    in_specs = (P(None, ("brow", "bcol", "freq"), None), P())
    out_specs = P(None, "freq", "brow", None, "bcol", None)
    return jax.shard_map(shards, mesh=mesh, in_specs=in_specs, out_specs=out_specs, check_vma=False)
```

```python
import functools
import math

import jax
import jax.numpy as jnp
import numpy as np
from jax import lax
from jax.experimental import pallas as pl
from jax.experimental.pallas import tpu as pltpu
from jax.sharding import PartitionSpec as P

CHANNELS = 4096
SCALE = 1.0 / 64.0
TAPS = 16
AVG = 32
FRAMES = 8
SLOW = 32
FAST = 128
WIDTH = 4
OWNED = 4
GROUPS = 32
N_SHIFTS = GROUPS - 1
LOADS = 2
SPAN = CHANNELS // LOADS
KEPT = FRAMES * SLOW
ROWS = 2 * WIDTH
N_X = 4
N_Z = 8
N_BCOL = 4
MESH = pl.DeviceIdType.MESH
F32 = jnp.float32
BF16 = jnp.bfloat16


def halves(table):
    high = table.astype(np.float32).astype(jnp.bfloat16)
    low = (table - high.astype(np.float64)).astype(np.float32).astype(jnp.bfloat16)
    return high, low


def tables():
    b, k1 = np.arange(SLOW), np.arange(SLOW)
    angle = 2.0 * np.pi * (np.outer(k1, b) % SLOW) / SLOW
    first = np.zeros((2, WIDTH, SLOW, SLOW, 2, WIDTH))
    for s in range(WIDTH):
        first[0, s, :, :, 0, s] = np.cos(angle)
        first[0, s, :, :, 1, s] = np.sin(angle)
        first[1, s, :, :, 0, s] = -np.sin(angle)
        first[1, s, :, :, 1, s] = np.cos(angle)
    first = first.reshape(256, 256)
    n, m = np.arange(FAST), np.arange(FAST)
    angle = 2.0 * np.pi * (np.outer(m, n) % FAST) / FAST
    second = np.zeros((FAST, 2, 2, FAST))
    second[:, 0, 0, :] = np.cos(angle)
    second[:, 0, 1, :] = np.sin(angle)
    second[:, 1, 0, :] = -np.sin(angle)
    second[:, 1, 1, :] = np.cos(angle)
    second = second.reshape(256, 256) * SCALE
    angle = 2.0 * np.pi * np.outer(k1, n) / CHANNELS
    turn = np.stack([np.cos(angle), np.sin(angle)]).astype(np.float32)
    sort = np.zeros((2, GROUPS, WIDTH, GROUPS, 2, WIDTH), np.float32)
    for d in range(2):
        for g in range(GROUPS):
            for s in range(WIDTH):
                sort[d, g, s, g, d, s] = 1.0
    sort = sort.reshape(256, 256).astype(jnp.bfloat16)
    return np.stack(halves(first)), np.stack(halves(second)), turn, sort


FIRST, SECOND, TURN, SORT = tables()
NT = (((1,), (1,)), ((), ()))


def split(value):
    high = value.astype(BF16)
    low = (value - high.astype(F32)).astype(BF16)
    return high, low


def channelize(x_ref, ready, tables_ready, taps_ref, first_ref, second_ref, turn_ref, spectra, fir, spread):
    def column(group, b, carry):
        lanes = pl.multiple_of(group * SPAN + b * FAST, FAST)
        rows = pl.multiple_of((group * (SPAN // FAST) + b) * ROWS, ROWS)
        frames = []
        for j in range(FRAMES + TAPS - 1):
            at = pl.ds(pl.multiple_of(j * SPAN + b * FAST, FAST), FAST)
            frames.append(jnp.concatenate([x_ref[group, c, :, at].astype(F32) for c in range(2)], axis=0))
        taps = [taps_ref[pl.ds(p, 1), pl.ds(lanes, FAST)] for p in range(TAPS)]
        for t in range(FRAMES):
            total = taps[0] * frames[t]
            for p in range(1, TAPS):
                total = total + taps[p] * frames[t + p]
            fir[pl.ds(rows, ROWS), t * FAST:(t + 1) * FAST] = total
        return carry

    for group in range(LOADS):
        ready(group)
        lax.fori_loop(0, SPAN // FAST, functools.partial(column, group), 0, unroll=4)
    tables_ready()
    high, low = split(fir[...])
    dot = functools.partial(jnp.dot, preferred_element_type=F32)
    section = dot(first_ref[0], high) + dot(first_ref[1], high) + dot(first_ref[0], low)
    cosine, sine = turn_ref[0], turn_ref[1]
    for s in range(WIDTH):
        parts = []
        for t in range(FRAMES):
            real = section[s * SLOW:(s + 1) * SLOW, t * FAST:(t + 1) * FAST]
            imag = section[128 + s * SLOW:128 + (s + 1) * SLOW, t * FAST:(t + 1) * FAST]
            parts.append(jnp.concatenate([real * cosine + imag * sine, imag * cosine - real * sine], axis=1))
        high, low = split(jnp.concatenate(parts, axis=0))
        dot_nt = functools.partial(lax.dot_general, dimension_numbers=NT, preferred_element_type=F32)
        spectrum = dot_nt(second_ref[0], high) + dot_nt(second_ref[1], high) + dot_nt(second_ref[0], low)
        for half in range(2):
            lanes = slice(half * 128, (half + 1) * 128)
            spread[half, pl.ds(s, 256, stride=WIDTH), :] = spectrum[:, lanes]
    for half in range(2):
        lanes = slice(half * 128, (half + 1) * 128)
        spectra[:, :, :, lanes] = spread[half].reshape(GROUPS, OWNED, ROWS, 128).astype(BF16)


SHIFTS = ((0, 1), (0, 3), (1, 0), (7, 0), (4, 2), (0, 2), (1, 1), (1, 3), (2, 0), (6, 0), (7, 1), (7, 3), (3, 2), (4, 1), (4, 3), (5, 2), (1, 2), (2, 1), (2, 3), (3, 0), (5, 0), (6, 1), (6, 3), (7, 2), (2, 2), (3, 1), (3, 3), (4, 0), (5, 1), (5, 3), (6, 2))
SCHEDULE = (('o', 0), ('o', 1), ('o', 2), ('n', 0), ('o', 3), ('n', 1), ('n', 5), ('o', 5), ('o', 6), ('o', 7), ('n', 2), ('o', 8), ('n', 3), ('o', 9), ('o', 10), ('o', 11), ('o', 4), ('n', 6), ('n', 7), ('n', 8), ('n', 9), ('o', 16), ('o', 12), ('n', 10), ('o', 17), ('o', 13), ('n', 11), ('o', 18), ('o', 14), ('n', 4), ('o', 19), ('o', 15), ('o', 20), ('o', 21), ('o', 22), ('o', 23), ('n', 16), ('n', 12), ('o', 24), ('n', 17), ('o', 25), ('n', 13), ('o', 26), ('n', 18), ('o', 27), ('n', 14), ('o', 28), ('n', 19), ('o', 29), ('n', 15), ('o', 30), ('n', 20), ('n', 21), ('n', 22), ('n', 23), ('n', 24), ('n', 25), ('n', 26), ('n', 27), ('n', 28), ('n', 29), ('n', 30))


def spectra_kernel(
    x_hbm, taps_hbm, first_hbm, second_hbm, turn_hbm, blocks, x_ref, taps_ref, first_ref, second_ref, turn_ref, fir, spread,
    spectra, load_sem, frame_sem, local, turn_send, turn_recv, near_send, core_send, relay_send, far_send, near_recv, core_recv,
    relay_recv, far_recv
):
    loads = [
        pltpu.make_async_copy(source, target, load_sem.at[i])
        for i, (source, target) in enumerate(
            ((taps_hbm, taps_ref), (first_hbm, first_ref), (second_hbm, second_ref), (turn_hbm, turn_ref))
        )
    ]
    loads[0].start()

    def load_frames(group):
        for j in range(FRAMES + TAPS - 1):
            pltpu.make_async_copy(
                x_hbm.at[:, :, pl.ds(j * CHANNELS + group * SPAN, SPAN)], x_ref.at[group, :, :, pl.ds(j * SPAN, SPAN)],
                frame_sem.at[group],
            ).start()

    for group in range(LOADS):
        load_frames(group)
    for copy in loads[1:]:
        copy.start()

    freq, brow, bcol = lax.axis_index("freq"), lax.axis_index("brow"), lax.axis_index("bcol")
    z, x = freq // N_X, freq % N_X
    y_low, core = bcol // 2, bcol % 2
    other_core = 2 * y_low + 1 - core
    near = 2 * (1 - y_low) + core

    barrier = pltpu.get_barrier_semaphore()

    def greet(i, carry):
        pl.semaphore_signal(barrier, inc=1, device_id=((freq + i) % GROUPS, brow, bcol), device_id_type=MESH)
        return carry

    lax.fori_loop(1, GROUPS, greet, 0)
    for peer in ((freq, brow, other_core), (freq, brow, near), (freq, 1 - brow, near)):
        pl.semaphore_signal(barrier, inc=1, device_id=peer, device_id_type=MESH)

    for dx in range(1, N_X):
        peer = (z * N_X + (x + dx) % N_X, brow, near)
        pl.semaphore_signal(barrier, inc=1, device_id=peer, device_id_type=MESH)

    loads[0].wait()

    def ready(group):
        pltpu.make_async_copy(x_ref.at[group], x_ref.at[group], frame_sem.at[group]).wait()

    def tables_ready():
        for copy in loads[1:]:
            copy.wait()

    channelize(x_ref, ready, tables_ready, taps_ref, first_ref, second_ref, turn_ref, spectra, fir, spread)
    pl.semaphore_wait(barrier, GROUPS - 1 + 3 + N_X - 1)

    def group_of(dz, dx):
        return (z + N_Z - dz) % N_Z * N_X + (x + N_X - dx) % N_X

    def row_of(slot, dz):
        return blocks.at[slot, :, pl.ds((z + N_Z - dz) % N_Z * N_X, N_X)]

    def send(source, target, peer, send_sem, recv_sem):
        pltpu.make_async_remote_copy(
            src_ref=source, dst_ref=target, send_sem=send_sem, recv_sem=recv_sem, device_id=peer, device_id_type=MESH
        ).start()

    def arrived(ref, semaphore):
        pltpu.make_async_copy(ref, ref, semaphore).wait()

    own = pltpu.make_async_copy(spectra.at[freq], blocks.at[bcol, :, freq], local)
    own.start()
    send(spectra.at[freq], blocks.at[bcol, :, freq], (freq, brow, near), near_send, near_recv.at[N_SHIFTS])
    for i, (dz, dx) in enumerate(SHIFTS):
        target = group_of(N_Z - dz, N_X - dx)
        send(spectra.at[target], blocks.at[bcol, :, freq], (target, brow, bcol), turn_send, turn_recv.at[i])
        if dz == 0:
            send(spectra.at[target], blocks.at[bcol, :, freq], (target, brow, near), near_send, near_recv.at[i])
    own.wait()
    held_own, held_near = [N_X] * N_Z, [N_X] * N_Z
    held_own[0] -= 1

    def take_own(i):
        dz, dx = SHIFTS[i]
        held = blocks.at[bcol, :, group_of(dz, dx)]
        arrived(held, turn_recv.at[i])
        if dz:
            send(held, held, (freq, brow, near), near_send, near_recv.at[i])
        held_own[dz] -= 1
        if not held_own[dz]:
            row = row_of(bcol, dz)
            send(row, row, (freq, brow, other_core), core_send, core_recv)

    def take_near(i):
        dz, dx = SHIFTS[i] if i < N_SHIFTS else (0, 0)
        group = group_of(dz, dx)
        held = blocks.at[near, :, group]
        arrived(held, near_recv.at[i])
        send(held, blocks.at[N_BCOL, :, group], (freq, 1 - brow, near), far_send, far_recv)
        held_near[dz] -= 1
        if not held_near[dz]:
            row = row_of(near, dz)
            send(row, row, (freq, brow, other_core), relay_send, relay_recv)

    take_near(N_SHIFTS)
    for kind, i in SCHEDULE:
        (take_own if kind == "o" else take_near)(i)
    arrived(spectra.at[pl.ds(0, GROUPS - 1)], turn_send)
    for semaphore in (near_send, core_send, relay_send, far_send, core_recv, relay_recv, far_recv):
        arrived(blocks.at[0], semaphore)


def spread_spectra(voltages, fir_taps):
    anywhere = pl.BlockSpec(memory_space=pl.ANY)
    dma = pltpu.SemaphoreType.DMA
    blocks = pl.pallas_call(
        spectra_kernel,
        out_shape=jax.ShapeDtypeStruct((N_BCOL + 1, OWNED, GROUPS, ROWS, KEPT), BF16),
        in_specs=[pl.BlockSpec(memory_space=pltpu.HBM)] * 5,
        out_specs=anywhere,
        scratch_shapes=[
            pltpu.VMEM((LOADS, 2, WIDTH, (FRAMES + TAPS - 1) * SPAN), BF16),
            pltpu.VMEM(fir_taps.shape, F32),
            pltpu.VMEM(FIRST.shape, BF16),
            pltpu.VMEM(SECOND.shape, BF16),
            pltpu.VMEM(TURN.shape, F32),
            pltpu.VMEM((256, FRAMES * FAST), F32),
            pltpu.VMEM((2, GROUPS * OWNED * ROWS, 128), F32),
            pltpu.VMEM((GROUPS, OWNED, ROWS, KEPT), BF16),
            dma((4,)), dma((LOADS,)), dma, dma, dma((N_SHIFTS,)), dma, dma, dma, dma, dma((N_SHIFTS + 1,)), dma, dma, dma,
        ],
        compiler_params=pltpu.CompilerParams(collective_id=0, has_side_effects=True, vmem_limit_bytes=24 * 2**20),
        name="spectra",
    )(*[pltpu.with_memory_space_constraint(v, pltpu.HBM) for v in (voltages, fir_taps, jnp.asarray(FIRST), jnp.asarray(SECOND), jnp.asarray(TURN))])
    return blocks.reshape(N_BCOL + 1, OWNED, GROUPS * ROWS, KEPT)


def correlate_kernel(held, sort_ref, out, built, store_sem):
    brow, bcol = lax.axis_index("brow"), lax.axis_index("bcol")
    slots = (bcol + brow * (N_BCOL - bcol), N_BCOL - brow * (N_BCOL - bcol))
    upper = lax.broadcasted_iota(jnp.int32, (GROUPS, ROWS, 256), 1) < WIDTH
    stores = []
    for q in range(OWNED):
        sort = sort_ref[...]
        parts = [jnp.dot(sort, held[slot, q], preferred_element_type=F32).astype(BF16) for slot in slots]
        right = jnp.concatenate([parts[0][:128], parts[1][:128], parts[0][128:], parts[1][128:]], axis=0)
        for block in range(N_BCOL):
            product = lax.dot_general(held[block, q], right, NT, preferred_element_type=F32)
            with_real = product[:, :256].reshape(GROUPS, ROWS, 256)
            with_imag = pltpu.roll(product[:, 256:].reshape(GROUPS, ROWS, 256), WIDTH, axis=1)
            mixed = (with_real + jnp.where(upper, with_imag, -with_imag)) * (1.0 / (FRAMES * AVG))
            pairs = mixed.reshape(GROUPS // 2, 2, ROWS, 256)
            even, odd = pairs[:, 0], pairs[:, 1]
            real = jnp.where(upper[:GROUPS // 2], even, pltpu.roll(odd, WIDTH, axis=1)).reshape(128, 256)
            imag = jnp.where(upper[:GROUPS // 2], pltpu.roll(even, WIDTH, axis=1), odd).reshape(128, 256)
            for r in range(2):
                rows = pl.ds(block * 256 + r, 128, stride=2)
                built[0, q, rows, :] = real[:, r * 128:(r + 1) * 128]
                built[1, q, rows, :] = imag[:, r * 128:(r + 1) * 128]
            part = (slice(None), q, pl.ds(block * 256, 256))
            stores.append(pltpu.make_async_copy(built.at[part], out.at[part], store_sem.at[q, block]))
            stores[-1].start()
    for copy in stores:
        copy.wait()


def correlate(blocks):
    vmem = pl.BlockSpec(memory_space=pltpu.VMEM)
    shape = (2, OWNED, 1024, 128)
    return pl.pallas_call(
        correlate_kernel,
        out_shape=jax.ShapeDtypeStruct(shape, F32),
        in_specs=[vmem] * 2,
        out_specs=pl.BlockSpec(memory_space=pltpu.HBM),
        scratch_shapes=[pltpu.VMEM(shape, F32), pltpu.SemaphoreType.DMA((OWNED, N_BCOL))],
        compiler_params=pltpu.CompilerParams(vmem_limit_bytes=24 * 2**20),
        name="correlate",
    )(blocks, jnp.asarray(SORT))


def shards(voltages, fir_taps):
    blocks = spread_spectra(voltages, fir_taps)
    return correlate(blocks).reshape(2, OWNED, 512, 2, 1, 128)


def solution(mesh):
    in_specs = (P(None, ("brow", "bcol", "freq"), None), P())
    out_specs = P(None, "freq", "brow", None, "bcol", None)
    return jax.shard_map(shards, mesh=mesh, in_specs=in_specs, out_specs=out_specs, check_vma=False)
```

```python
import functools
import math

import jax
import jax.numpy as jnp
import numpy as np
from jax import lax
from jax.experimental import pallas as pl
from jax.experimental.pallas import tpu as pltpu
from jax.sharding import PartitionSpec as P

CHANNELS = 4096
SCALE = 1.0 / 64.0
TAPS = 16
AVG = 32
FRAMES = 8
SLOW = 32
FAST = 128
WIDTH = 4
OWNED = 4
GROUPS = 32
N_SHIFTS = GROUPS - 1
LOADS = 2
SPAN = CHANNELS // LOADS
KEPT = FRAMES * SLOW
ROWS = 2 * WIDTH
N_X = 4
N_Z = 8
N_BCOL = 4
MESH = pl.DeviceIdType.MESH
F32 = jnp.float32
BF16 = jnp.bfloat16


def halves(table):
    high = table.astype(np.float32).astype(jnp.bfloat16)
    low = (table - high.astype(np.float64)).astype(np.float32).astype(jnp.bfloat16)
    return high, low


def tables():
    b, k1 = np.arange(SLOW), np.arange(SLOW)
    angle = 2.0 * np.pi * (np.outer(k1, b) % SLOW) / SLOW
    first = np.zeros((2, WIDTH, SLOW, SLOW, 2, WIDTH))
    for s in range(WIDTH):
        first[0, s, :, :, 0, s] = np.cos(angle)
        first[0, s, :, :, 1, s] = np.sin(angle)
        first[1, s, :, :, 0, s] = -np.sin(angle)
        first[1, s, :, :, 1, s] = np.cos(angle)
    first = first.reshape(256, 256)
    n, m = np.arange(FAST), np.arange(FAST)
    angle = 2.0 * np.pi * (np.outer(m, n) % FAST) / FAST
    second = np.zeros((FAST, 2, 2, FAST))
    second[:, 0, 0, :] = np.cos(angle)
    second[:, 0, 1, :] = np.sin(angle)
    second[:, 1, 0, :] = -np.sin(angle)
    second[:, 1, 1, :] = np.cos(angle)
    second = second.reshape(256, 256) * SCALE
    angle = 2.0 * np.pi * np.outer(k1, n) / CHANNELS
    turn = np.stack([np.cos(angle), np.sin(angle)]).astype(np.float32)
    sort = np.zeros((2, GROUPS, WIDTH, GROUPS, 2, WIDTH), np.float32)
    for d in range(2):
        for g in range(GROUPS):
            for s in range(WIDTH):
                sort[d, g, s, g, d, s] = 1.0
    sort = sort.reshape(256, 256).astype(jnp.bfloat16)
    return np.stack(halves(first)), np.stack(halves(second)), turn, sort


FIRST, SECOND, TURN, SORT = tables()
NT = (((1,), (1,)), ((), ()))


def split(value):
    high = value.astype(BF16)
    low = (value - high.astype(F32)).astype(BF16)
    return high, low


def channelize(x_ref, ready, tables_ready, taps_ref, first_ref, second_ref, turn_ref, spectra, fir, spread):
    def column(group, b, carry):
        lanes = pl.multiple_of(group * SPAN + b * FAST, FAST)
        rows = pl.multiple_of((group * (SPAN // FAST) + b) * ROWS, ROWS)
        frames = []
        for j in range(FRAMES + TAPS - 1):
            at = pl.ds(pl.multiple_of(j * SPAN + b * FAST, FAST), FAST)
            frames.append(jnp.concatenate([x_ref[group, c, :, at].astype(F32) for c in range(2)], axis=0))
        taps = [taps_ref[pl.ds(p, 1), pl.ds(lanes, FAST)] for p in range(TAPS)]
        for t in range(FRAMES):
            total = taps[0] * frames[t]
            for p in range(1, TAPS):
                total = total + taps[p] * frames[t + p]
            fir[pl.ds(rows, ROWS), t * FAST:(t + 1) * FAST] = total
        return carry

    for group in range(LOADS):
        ready(group)
        lax.fori_loop(0, SPAN // FAST, functools.partial(column, group), 0, unroll=4)
    tables_ready()
    high, low = split(fir[...])
    dot = functools.partial(jnp.dot, preferred_element_type=F32)
    section = dot(first_ref[0], high) + dot(first_ref[1], high) + dot(first_ref[0], low)
    cosine, sine = turn_ref[0], turn_ref[1]
    for s in range(WIDTH):
        parts = []
        for t in range(FRAMES):
            real = section[s * SLOW:(s + 1) * SLOW, t * FAST:(t + 1) * FAST]
            imag = section[128 + s * SLOW:128 + (s + 1) * SLOW, t * FAST:(t + 1) * FAST]
            parts.append(jnp.concatenate([real * cosine + imag * sine, imag * cosine - real * sine], axis=1))
        high, low = split(jnp.concatenate(parts, axis=0))
        dot_nt = functools.partial(lax.dot_general, dimension_numbers=NT, preferred_element_type=F32)
        spectrum = dot_nt(second_ref[0], high) + dot_nt(second_ref[1], high) + dot_nt(second_ref[0], low)
        for half in range(2):
            lanes = slice(half * 128, (half + 1) * 128)
            spread[half, pl.ds(s, 256, stride=WIDTH), :] = spectrum[:, lanes]
    for half in range(2):
        lanes = slice(half * 128, (half + 1) * 128)
        spectra[:, :, :, lanes] = spread[half].reshape(GROUPS, OWNED, ROWS, 128).astype(BF16)


SHIFTS = ((0, 1), (0, 3), (1, 0), (7, 0), (0, 2), (1, 1), (1, 3), (2, 0), (6, 0), (7, 1), (7, 3), (4, 2), (3, 2), (4, 1), (4, 3), (5, 2), (1, 2), (2, 1), (2, 3), (3, 0), (5, 0), (6, 1), (6, 3), (7, 2), (2, 2), (3, 1), (3, 3), (4, 0), (5, 1), (5, 3), (6, 2))
SCHEDULE = (('o', 0), ('o', 1), ('o', 2), ('n', 0), ('o', 3), ('n', 1), ('n', 4), ('o', 4), ('o', 5), ('o', 6), ('o', 7), ('n', 2), ('o', 8), ('n', 3), ('o', 9), ('o', 10), ('n', 5), ('n', 6), ('n', 7), ('n', 8), ('n', 9), ('o', 16), ('o', 12), ('n', 10), ('o', 17), ('o', 13), ('o', 11), ('o', 18), ('o', 14), ('o', 19), ('o', 15), ('o', 20), ('o', 21), ('o', 22), ('o', 23), ('n', 16), ('n', 12), ('o', 24), ('n', 17), ('o', 25), ('n', 13), ('o', 26), ('n', 11), ('o', 27), ('n', 18), ('o', 28), ('n', 14), ('o', 29), ('n', 19), ('o', 30), ('n', 15), ('n', 20), ('n', 21), ('n', 22), ('n', 23), ('n', 24), ('n', 25), ('n', 26), ('n', 27), ('n', 28), ('n', 29), ('n', 30))


def spectra_kernel(
    x_hbm, taps_hbm, first_hbm, second_hbm, turn_hbm, blocks, x_ref, taps_ref, first_ref, second_ref, turn_ref, fir, spread,
    spectra, load_sem, frame_sem, local, turn_send, turn_recv, near_send, core_send, relay_send, far_send, near_recv, core_recv,
    relay_recv, far_recv
):
    loads = [
        pltpu.make_async_copy(source, target, load_sem.at[i])
        for i, (source, target) in enumerate(
            ((taps_hbm, taps_ref), (first_hbm, first_ref), (second_hbm, second_ref), (turn_hbm, turn_ref))
        )
    ]
    loads[0].start()

    def load_frames(group):
        for j in range(FRAMES + TAPS - 1):
            pltpu.make_async_copy(
                x_hbm.at[:, :, pl.ds(j * CHANNELS + group * SPAN, SPAN)], x_ref.at[group, :, :, pl.ds(j * SPAN, SPAN)],
                frame_sem.at[group],
            ).start()

    for group in range(LOADS):
        load_frames(group)
    for copy in loads[1:]:
        copy.start()

    freq, brow, bcol = lax.axis_index("freq"), lax.axis_index("brow"), lax.axis_index("bcol")
    z, x = freq // N_X, freq % N_X
    y_low, core = bcol // 2, bcol % 2
    other_core = 2 * y_low + 1 - core
    near = 2 * (1 - y_low) + core

    barrier = pltpu.get_barrier_semaphore()

    def greet(i, carry):
        pl.semaphore_signal(barrier, inc=1, device_id=((freq + i) % GROUPS, brow, bcol), device_id_type=MESH)
        return carry

    lax.fori_loop(1, GROUPS, greet, 0)
    for peer in ((freq, brow, other_core), (freq, brow, near), (freq, 1 - brow, near)):
        pl.semaphore_signal(barrier, inc=1, device_id=peer, device_id_type=MESH)

    for dx in range(1, N_X):
        peer = (z * N_X + (x + dx) % N_X, brow, near)
        pl.semaphore_signal(barrier, inc=1, device_id=peer, device_id_type=MESH)

    loads[0].wait()

    def ready(group):
        pltpu.make_async_copy(x_ref.at[group], x_ref.at[group], frame_sem.at[group]).wait()

    def tables_ready():
        for copy in loads[1:]:
            copy.wait()

    channelize(x_ref, ready, tables_ready, taps_ref, first_ref, second_ref, turn_ref, spectra, fir, spread)
    pl.semaphore_wait(barrier, GROUPS - 1 + 3 + N_X - 1)

    def group_of(dz, dx):
        return (z + N_Z - dz) % N_Z * N_X + (x + N_X - dx) % N_X

    def row_of(slot, dz):
        return blocks.at[slot, :, pl.ds((z + N_Z - dz) % N_Z * N_X, N_X)]

    def send(source, target, peer, send_sem, recv_sem):
        pltpu.make_async_remote_copy(
            src_ref=source, dst_ref=target, send_sem=send_sem, recv_sem=recv_sem, device_id=peer, device_id_type=MESH
        ).start()

    def arrived(ref, semaphore):
        pltpu.make_async_copy(ref, ref, semaphore).wait()

    own = pltpu.make_async_copy(spectra.at[freq], blocks.at[bcol, :, freq], local)
    own.start()
    send(spectra.at[freq], blocks.at[bcol, :, freq], (freq, brow, near), near_send, near_recv.at[N_SHIFTS])
    for i, (dz, dx) in enumerate(SHIFTS):
        target = group_of(N_Z - dz, N_X - dx)
        send(spectra.at[target], blocks.at[bcol, :, freq], (target, brow, bcol), turn_send, turn_recv.at[i])
        if dz == 0:
            send(spectra.at[target], blocks.at[bcol, :, freq], (target, brow, near), near_send, near_recv.at[i])
    own.wait()
    held_own, held_near = [N_X] * N_Z, [N_X] * N_Z
    held_own[0] -= 1

    def take_own(i):
        dz, dx = SHIFTS[i]
        held = blocks.at[bcol, :, group_of(dz, dx)]
        arrived(held, turn_recv.at[i])
        if dz:
            send(held, held, (freq, brow, near), near_send, near_recv.at[i])
        held_own[dz] -= 1
        if not held_own[dz]:
            row = row_of(bcol, dz)
            send(row, row, (freq, brow, other_core), core_send, core_recv)

    def take_near(i):
        dz, dx = SHIFTS[i] if i < N_SHIFTS else (0, 0)
        group = group_of(dz, dx)
        held = blocks.at[near, :, group]
        arrived(held, near_recv.at[i])
        send(held, blocks.at[N_BCOL, :, group], (freq, 1 - brow, near), far_send, far_recv)
        held_near[dz] -= 1
        if not held_near[dz]:
            row = row_of(near, dz)
            send(row, row, (freq, brow, other_core), relay_send, relay_recv)

    take_near(N_SHIFTS)
    for kind, i in SCHEDULE:
        (take_own if kind == "o" else take_near)(i)
    arrived(spectra.at[pl.ds(0, GROUPS - 1)], turn_send)
    for semaphore in (near_send, core_send, relay_send, far_send, core_recv, relay_recv, far_recv):
        arrived(blocks.at[0], semaphore)


def spread_spectra(voltages, fir_taps):
    anywhere = pl.BlockSpec(memory_space=pl.ANY)
    dma = pltpu.SemaphoreType.DMA
    blocks = pl.pallas_call(
        spectra_kernel,
        out_shape=jax.ShapeDtypeStruct((N_BCOL + 1, OWNED, GROUPS, ROWS, KEPT), BF16),
        in_specs=[pl.BlockSpec(memory_space=pltpu.HBM)] * 5,
        out_specs=anywhere,
        scratch_shapes=[
            pltpu.VMEM((LOADS, 2, WIDTH, (FRAMES + TAPS - 1) * SPAN), BF16),
            pltpu.VMEM(fir_taps.shape, F32),
            pltpu.VMEM(FIRST.shape, BF16),
            pltpu.VMEM(SECOND.shape, BF16),
            pltpu.VMEM(TURN.shape, F32),
            pltpu.VMEM((256, FRAMES * FAST), F32),
            pltpu.VMEM((2, GROUPS * OWNED * ROWS, 128), F32),
            pltpu.VMEM((GROUPS, OWNED, ROWS, KEPT), BF16),
            dma((4,)), dma((LOADS,)), dma, dma, dma((N_SHIFTS,)), dma, dma, dma, dma, dma((N_SHIFTS + 1,)), dma, dma, dma,
        ],
        compiler_params=pltpu.CompilerParams(collective_id=0, has_side_effects=True, vmem_limit_bytes=24 * 2**20),
        name="spectra",
    )(*[pltpu.with_memory_space_constraint(v, pltpu.HBM) for v in (voltages, fir_taps, jnp.asarray(FIRST), jnp.asarray(SECOND), jnp.asarray(TURN))])
    return blocks.reshape(N_BCOL + 1, OWNED, GROUPS * ROWS, KEPT)


def correlate_kernel(held, sort_ref, out, built, store_sem):
    brow, bcol = lax.axis_index("brow"), lax.axis_index("bcol")
    slots = (bcol + brow * (N_BCOL - bcol), N_BCOL - brow * (N_BCOL - bcol))
    upper = lax.broadcasted_iota(jnp.int32, (GROUPS, ROWS, 256), 1) < WIDTH
    stores = []
    for q in range(OWNED):
        sort = sort_ref[...]
        parts = [jnp.dot(sort, held[slot, q], preferred_element_type=F32).astype(BF16) for slot in slots]
        right = jnp.concatenate([parts[0][:128], parts[1][:128], parts[0][128:], parts[1][128:]], axis=0)
        for block in range(N_BCOL):
            product = lax.dot_general(held[block, q], right, NT, preferred_element_type=F32)
            with_real = product[:, :256].reshape(GROUPS, ROWS, 256)
            with_imag = pltpu.roll(product[:, 256:].reshape(GROUPS, ROWS, 256), WIDTH, axis=1)
            mixed = (with_real + jnp.where(upper, with_imag, -with_imag)) * (1.0 / (FRAMES * AVG))
            pairs = mixed.reshape(GROUPS // 2, 2, ROWS, 256)
            even, odd = pairs[:, 0], pairs[:, 1]
            real = jnp.where(upper[:GROUPS // 2], even, pltpu.roll(odd, WIDTH, axis=1)).reshape(128, 256)
            imag = jnp.where(upper[:GROUPS // 2], pltpu.roll(even, WIDTH, axis=1), odd).reshape(128, 256)
            for r in range(2):
                rows = pl.ds(block * 256 + r, 128, stride=2)
                built[0, q, rows, :] = real[:, r * 128:(r + 1) * 128]
                built[1, q, rows, :] = imag[:, r * 128:(r + 1) * 128]
            part = (slice(None), q, pl.ds(block * 256, 256))
            stores.append(pltpu.make_async_copy(built.at[part], out.at[part], store_sem.at[q, block]))
            stores[-1].start()
    for copy in stores:
        copy.wait()


def correlate(blocks):
    vmem = pl.BlockSpec(memory_space=pltpu.VMEM)
    shape = (2, OWNED, 1024, 128)
    return pl.pallas_call(
        correlate_kernel,
        out_shape=jax.ShapeDtypeStruct(shape, F32),
        in_specs=[vmem] * 2,
        out_specs=pl.BlockSpec(memory_space=pltpu.HBM),
        scratch_shapes=[pltpu.VMEM(shape, F32), pltpu.SemaphoreType.DMA((OWNED, N_BCOL))],
        compiler_params=pltpu.CompilerParams(vmem_limit_bytes=24 * 2**20),
        name="correlate",
    )(blocks, jnp.asarray(SORT))


def shards(voltages, fir_taps):
    blocks = spread_spectra(voltages, fir_taps)
    return correlate(blocks).reshape(2, OWNED, 512, 2, 1, 128)


def solution(mesh):
    in_specs = (P(None, ("brow", "bcol", "freq"), None), P())
    out_specs = P(None, "freq", "brow", None, "bcol", None)
    return jax.shard_map(shards, mesh=mesh, in_specs=in_specs, out_specs=out_specs, check_vma=False)
```

```python
import functools
import math

import jax
import jax.numpy as jnp
import numpy as np
from jax import lax
from jax.experimental import pallas as pl
from jax.experimental.pallas import tpu as pltpu
from jax.sharding import PartitionSpec as P

CHANNELS = 4096
SCALE = 1.0 / 64.0
TAPS = 16
AVG = 32
FRAMES = 8
SLOW = 32
FAST = 128
WIDTH = 4
OWNED = 4
GROUPS = 32
N_SHIFTS = GROUPS - 1
LOADS = 4
SPAN = CHANNELS // LOADS
KEPT = FRAMES * SLOW
ROWS = 2 * WIDTH
N_X = 4
N_Z = 8
N_BCOL = 4
MESH = pl.DeviceIdType.MESH
F32 = jnp.float32
BF16 = jnp.bfloat16


def halves(table):
    high = table.astype(np.float32).astype(jnp.bfloat16)
    low = (table - high.astype(np.float64)).astype(np.float32).astype(jnp.bfloat16)
    return high, low


def tables():
    b, k1 = np.arange(SLOW), np.arange(SLOW)
    angle = 2.0 * np.pi * (np.outer(k1, b) % SLOW) / SLOW
    first = np.zeros((2, WIDTH, SLOW, SLOW, 2, WIDTH))
    for s in range(WIDTH):
        first[0, s, :, :, 0, s] = np.cos(angle)
        first[0, s, :, :, 1, s] = np.sin(angle)
        first[1, s, :, :, 0, s] = -np.sin(angle)
        first[1, s, :, :, 1, s] = np.cos(angle)
    first = first.reshape(256, 256)
    n, m = np.arange(FAST), np.arange(FAST)
    angle = 2.0 * np.pi * (np.outer(m, n) % FAST) / FAST
    second = np.zeros((FAST, 2, 2, FAST))
    second[:, 0, 0, :] = np.cos(angle)
    second[:, 0, 1, :] = np.sin(angle)
    second[:, 1, 0, :] = -np.sin(angle)
    second[:, 1, 1, :] = np.cos(angle)
    second = second.reshape(256, 256) * SCALE
    angle = 2.0 * np.pi * np.outer(k1, n) / CHANNELS
    turn = np.stack([np.cos(angle), np.sin(angle)]).astype(np.float32)
    sort = np.zeros((2, GROUPS, WIDTH, GROUPS, 2, WIDTH), np.float32)
    for d in range(2):
        for g in range(GROUPS):
            for s in range(WIDTH):
                sort[d, g, s, g, d, s] = 1.0
    sort = sort.reshape(256, 256).astype(jnp.bfloat16)
    return np.stack(halves(first)), np.stack(halves(second)), turn, sort


FIRST, SECOND, TURN, SORT = tables()
NT = (((1,), (1,)), ((), ()))


def split(value):
    high = value.astype(BF16)
    low = (value - high.astype(F32)).astype(BF16)
    return high, low


def channelize(x_ref, ready, tables_ready, taps_ref, first_ref, second_ref, turn_ref, spectra, fir, spread):
    def column(group, b, carry):
        lanes = pl.multiple_of(group * SPAN + b * FAST, FAST)
        rows = pl.multiple_of((group * (SPAN // FAST) + b) * ROWS, ROWS)
        frames = []
        for j in range(FRAMES + TAPS - 1):
            at = pl.ds(pl.multiple_of(j * SPAN + b * FAST, FAST), FAST)
            frames.append(jnp.concatenate([x_ref[group, c, :, at].astype(F32) for c in range(2)], axis=0))
        taps = [taps_ref[pl.ds(p, 1), pl.ds(lanes, FAST)] for p in range(TAPS)]
        for t in range(FRAMES):
            total = taps[0] * frames[t]
            for p in range(1, TAPS):
                total = total + taps[p] * frames[t + p]
            fir[pl.ds(rows, ROWS), t * FAST:(t + 1) * FAST] = total
        return carry

    for group in range(LOADS):
        ready(group)
        lax.fori_loop(0, SPAN // FAST, functools.partial(column, group), 0, unroll=8)
    tables_ready()
    high, low = split(fir[...])
    dot = functools.partial(jnp.dot, preferred_element_type=F32)
    section = dot(first_ref[0], high) + dot(first_ref[1], high) + dot(first_ref[0], low)
    cosine, sine = turn_ref[0], turn_ref[1]
    for s in range(WIDTH):
        parts = []
        for t in range(FRAMES):
            real = section[s * SLOW:(s + 1) * SLOW, t * FAST:(t + 1) * FAST]
            imag = section[128 + s * SLOW:128 + (s + 1) * SLOW, t * FAST:(t + 1) * FAST]
            parts.append(jnp.concatenate([real * cosine + imag * sine, imag * cosine - real * sine], axis=1))
        high, low = split(jnp.concatenate(parts, axis=0))
        dot_nt = functools.partial(lax.dot_general, dimension_numbers=NT, preferred_element_type=F32)
        spectrum = dot_nt(second_ref[0], high) + dot_nt(second_ref[1], high) + dot_nt(second_ref[0], low)
        for half in range(2):
            lanes = slice(half * 128, (half + 1) * 128)
            spread[half, pl.ds(s, 256, stride=WIDTH), :] = spectrum[:, lanes]
    for half in range(2):
        lanes = slice(half * 128, (half + 1) * 128)
        spectra[:, :, :, lanes] = spread[half].reshape(GROUPS, OWNED, ROWS, 128).astype(BF16)


SHIFTS = ((0, 1), (0, 3), (1, 0), (7, 0), (0, 2), (1, 1), (1, 3), (2, 0), (6, 0), (7, 1), (7, 3), (4, 2), (3, 2), (4, 1), (4, 3), (5, 2), (1, 2), (2, 1), (2, 3), (3, 0), (5, 0), (6, 1), (6, 3), (7, 2), (2, 2), (3, 1), (3, 3), (4, 0), (5, 1), (5, 3), (6, 2))
SCHEDULE = (('o', 0), ('o', 1), ('o', 2), ('n', 0), ('o', 3), ('n', 1), ('n', 4), ('o', 4), ('o', 5), ('o', 6), ('o', 7), ('n', 2), ('o', 8), ('n', 3), ('o', 9), ('o', 10), ('n', 5), ('n', 6), ('n', 7), ('n', 8), ('n', 9), ('o', 16), ('o', 12), ('n', 10), ('o', 17), ('o', 13), ('o', 11), ('o', 18), ('o', 14), ('o', 19), ('o', 15), ('o', 20), ('o', 21), ('o', 22), ('o', 23), ('n', 16), ('n', 12), ('o', 24), ('n', 17), ('o', 25), ('n', 13), ('o', 26), ('n', 11), ('o', 27), ('n', 18), ('o', 28), ('n', 14), ('o', 29), ('n', 19), ('o', 30), ('n', 15), ('n', 20), ('n', 21), ('n', 22), ('n', 23), ('n', 24), ('n', 25), ('n', 26), ('n', 27), ('n', 28), ('n', 29), ('n', 30))


def spectra_kernel(
    x_hbm, taps_hbm, first_hbm, second_hbm, turn_hbm, blocks, x_ref, taps_ref, first_ref, second_ref, turn_ref, fir, spread,
    spectra, load_sem, frame_sem, local, turn_send, turn_recv, near_send, core_send, relay_send, far_send, near_recv, core_recv,
    relay_recv, far_recv
):
    loads = [
        pltpu.make_async_copy(source, target, load_sem.at[i])
        for i, (source, target) in enumerate(
            ((taps_hbm, taps_ref), (first_hbm, first_ref), (second_hbm, second_ref), (turn_hbm, turn_ref))
        )
    ]
    loads[0].start()

    def load_frames(group):
        for j in range(FRAMES + TAPS - 1):
            pltpu.make_async_copy(
                x_hbm.at[:, :, pl.ds(j * CHANNELS + group * SPAN, SPAN)], x_ref.at[group, :, :, pl.ds(j * SPAN, SPAN)],
                frame_sem.at[group],
            ).start()

    for group in range(LOADS):
        load_frames(group)
    for copy in loads[1:]:
        copy.start()

    freq, brow, bcol = lax.axis_index("freq"), lax.axis_index("brow"), lax.axis_index("bcol")
    z, x = freq // N_X, freq % N_X
    y_low, core = bcol // 2, bcol % 2
    other_core = 2 * y_low + 1 - core
    near = 2 * (1 - y_low) + core

    barrier = pltpu.get_barrier_semaphore()

    def greet(i, carry):
        pl.semaphore_signal(barrier, inc=1, device_id=((freq + i) % GROUPS, brow, bcol), device_id_type=MESH)
        return carry

    lax.fori_loop(1, GROUPS, greet, 0)
    for peer in ((freq, brow, other_core), (freq, brow, near), (freq, 1 - brow, near)):
        pl.semaphore_signal(barrier, inc=1, device_id=peer, device_id_type=MESH)

    for dx in range(1, N_X):
        peer = (z * N_X + (x + dx) % N_X, brow, near)
        pl.semaphore_signal(barrier, inc=1, device_id=peer, device_id_type=MESH)

    loads[0].wait()

    def ready(group):
        pltpu.make_async_copy(x_ref.at[group], x_ref.at[group], frame_sem.at[group]).wait()

    def tables_ready():
        for copy in loads[1:]:
            copy.wait()

    channelize(x_ref, ready, tables_ready, taps_ref, first_ref, second_ref, turn_ref, spectra, fir, spread)
    pl.semaphore_wait(barrier, GROUPS - 1 + 3 + N_X - 1)

    def group_of(dz, dx):
        return (z + N_Z - dz) % N_Z * N_X + (x + N_X - dx) % N_X

    def row_of(slot, dz):
        return blocks.at[slot, :, pl.ds((z + N_Z - dz) % N_Z * N_X, N_X)]

    def send(source, target, peer, send_sem, recv_sem):
        pltpu.make_async_remote_copy(
            src_ref=source, dst_ref=target, send_sem=send_sem, recv_sem=recv_sem, device_id=peer, device_id_type=MESH
        ).start()

    def arrived(ref, semaphore):
        pltpu.make_async_copy(ref, ref, semaphore).wait()

    own = pltpu.make_async_copy(spectra.at[freq], blocks.at[bcol, :, freq], local)
    own.start()
    send(spectra.at[freq], blocks.at[bcol, :, freq], (freq, brow, near), near_send, near_recv.at[N_SHIFTS])
    for i, (dz, dx) in enumerate(SHIFTS):
        target = group_of(N_Z - dz, N_X - dx)
        send(spectra.at[target], blocks.at[bcol, :, freq], (target, brow, bcol), turn_send, turn_recv.at[i])
        if dz == 0:
            send(spectra.at[target], blocks.at[bcol, :, freq], (target, brow, near), near_send, near_recv.at[i])
    own.wait()
    held_own, held_near = [N_X] * N_Z, [N_X] * N_Z
    held_own[0] -= 1

    def take_own(i):
        dz, dx = SHIFTS[i]
        held = blocks.at[bcol, :, group_of(dz, dx)]
        arrived(held, turn_recv.at[i])
        if dz:
            send(held, held, (freq, brow, near), near_send, near_recv.at[i])
        held_own[dz] -= 1
        if not held_own[dz]:
            row = row_of(bcol, dz)
            send(row, row, (freq, brow, other_core), core_send, core_recv)

    def take_near(i):
        dz, dx = SHIFTS[i] if i < N_SHIFTS else (0, 0)
        group = group_of(dz, dx)
        held = blocks.at[near, :, group]
        arrived(held, near_recv.at[i])
        send(held, blocks.at[N_BCOL, :, group], (freq, 1 - brow, near), far_send, far_recv)
        held_near[dz] -= 1
        if not held_near[dz]:
            row = row_of(near, dz)
            send(row, row, (freq, brow, other_core), relay_send, relay_recv)

    take_near(N_SHIFTS)
    for kind, i in SCHEDULE:
        (take_own if kind == "o" else take_near)(i)
    arrived(spectra.at[pl.ds(0, GROUPS - 1)], turn_send)
    for semaphore in (near_send, core_send, relay_send, far_send, core_recv, relay_recv, far_recv):
        arrived(blocks.at[0], semaphore)


def spread_spectra(voltages, fir_taps):
    anywhere = pl.BlockSpec(memory_space=pl.ANY)
    dma = pltpu.SemaphoreType.DMA
    blocks = pl.pallas_call(
        spectra_kernel,
        out_shape=jax.ShapeDtypeStruct((N_BCOL + 1, OWNED, GROUPS, ROWS, KEPT), BF16),
        in_specs=[pl.BlockSpec(memory_space=pltpu.HBM)] * 5,
        out_specs=anywhere,
        scratch_shapes=[
            pltpu.VMEM((LOADS, 2, WIDTH, (FRAMES + TAPS - 1) * SPAN), BF16),
            pltpu.VMEM(fir_taps.shape, F32),
            pltpu.VMEM(FIRST.shape, BF16),
            pltpu.VMEM(SECOND.shape, BF16),
            pltpu.VMEM(TURN.shape, F32),
            pltpu.VMEM((256, FRAMES * FAST), F32),
            pltpu.VMEM((2, GROUPS * OWNED * ROWS, 128), F32),
            pltpu.VMEM((GROUPS, OWNED, ROWS, KEPT), BF16),
            dma((4,)), dma((LOADS,)), dma, dma, dma((N_SHIFTS,)), dma, dma, dma, dma, dma((N_SHIFTS + 1,)), dma, dma, dma,
        ],
        compiler_params=pltpu.CompilerParams(collective_id=0, has_side_effects=True, vmem_limit_bytes=24 * 2**20),
        name="spectra",
    )(*[pltpu.with_memory_space_constraint(v, pltpu.HBM) for v in (voltages, fir_taps, jnp.asarray(FIRST), jnp.asarray(SECOND), jnp.asarray(TURN))])
    return blocks.reshape(N_BCOL + 1, OWNED, GROUPS * ROWS, KEPT)


def correlate_kernel(held, sort_ref, out, built, store_sem):
    brow, bcol = lax.axis_index("brow"), lax.axis_index("bcol")
    slots = (bcol + brow * (N_BCOL - bcol), N_BCOL - brow * (N_BCOL - bcol))
    upper = lax.broadcasted_iota(jnp.int32, (GROUPS, ROWS, 256), 1) < WIDTH
    stores = []
    for q in range(OWNED):
        sort = sort_ref[...]
        parts = [jnp.dot(sort, held[slot, q], preferred_element_type=F32).astype(BF16) for slot in slots]
        right = jnp.concatenate([parts[0][:128], parts[1][:128], parts[0][128:], parts[1][128:]], axis=0)
        for block in range(N_BCOL):
            product = lax.dot_general(held[block, q], right, NT, preferred_element_type=F32)
            with_real = product[:, :256].reshape(GROUPS, ROWS, 256)
            with_imag = pltpu.roll(product[:, 256:].reshape(GROUPS, ROWS, 256), WIDTH, axis=1)
            mixed = (with_real + jnp.where(upper, with_imag, -with_imag)) * (1.0 / (FRAMES * AVG))
            pairs = mixed.reshape(GROUPS // 2, 2, ROWS, 256)
            even, odd = pairs[:, 0], pairs[:, 1]
            real = jnp.where(upper[:GROUPS // 2], even, pltpu.roll(odd, WIDTH, axis=1)).reshape(128, 256)
            imag = jnp.where(upper[:GROUPS // 2], pltpu.roll(even, WIDTH, axis=1), odd).reshape(128, 256)
            for r in range(2):
                rows = pl.ds(block * 256 + r, 128, stride=2)
                built[0, q, rows, :] = real[:, r * 128:(r + 1) * 128]
                built[1, q, rows, :] = imag[:, r * 128:(r + 1) * 128]
            part = (slice(None), q, pl.ds(block * 256, 256))
            stores.append(pltpu.make_async_copy(built.at[part], out.at[part], store_sem.at[q, block]))
            stores[-1].start()
    for copy in stores:
        copy.wait()


def correlate(blocks):
    vmem = pl.BlockSpec(memory_space=pltpu.VMEM)
    shape = (2, OWNED, 1024, 128)
    return pl.pallas_call(
        correlate_kernel,
        out_shape=jax.ShapeDtypeStruct(shape, F32),
        in_specs=[vmem] * 2,
        out_specs=pl.BlockSpec(memory_space=pltpu.HBM),
        scratch_shapes=[pltpu.VMEM(shape, F32), pltpu.SemaphoreType.DMA((OWNED, N_BCOL))],
        compiler_params=pltpu.CompilerParams(vmem_limit_bytes=24 * 2**20),
        name="correlate",
    )(blocks, jnp.asarray(SORT))


def shards(voltages, fir_taps):
    blocks = spread_spectra(voltages, fir_taps)
    return correlate(blocks).reshape(2, OWNED, 512, 2, 1, 128)


def solution(mesh):
    in_specs = (P(None, ("brow", "bcol", "freq"), None), P())
    out_specs = P(None, "freq", "brow", None, "bcol", None)
    return jax.shard_map(shards, mesh=mesh, in_specs=in_specs, out_specs=out_specs, check_vma=False)
```
